256 devices in a mesh: grid: 32 (over y_hi, z, core), orb: 8 (over y_lo, x).
Axes of the slice: x: 4, y: 4 (y_hi: 2, y_lo: 2; y = y_hi * 2 + y_lo), z: 8, core: 2. Of those that a mesh axis runs over, the one named last changes fastest.
Arguments:
- orbitals: float32 [64, 384, 4096], P('grid', 'orb'), may hold values from -6 to 6
- potential: float32 [64, 4096], P('grid'), may hold values from -4 to 4
- projectors: float32 [64, 256, 4096], P('grid', None, 'orb'), may hold values from -0.09375 to 0.09375
Outputs:
- filtered: float32 [64, 384, 4096], P('grid', 'orb')
The draws below stay inside these ranges and needn't reach their ends.
All inputs are finite; a program needn't handle non-finite values.
Results may differ from the reference program's by a relative error of at most 0.000084.
Values sent between devices are 32-bit elements; how exact they have to be, the bound alone decides.
A program may use at most 128 MiB of HBM per device.

```python
import jax
import jax.numpy as jnp
from jax import lax

NX = 64
NY = 64
NPROJ = 256
NXY = 4096
NZ = 64
NORB = 384


def shard_levels(key, dims, shards, smallest, high):
    def one(axis_at, blocks):
        steps = jax.random.uniform(jax.random.fold_in(jax.random.fold_in(key, 6), axis_at), (blocks,), jnp.float32, smallest / len(shards), high / len(shards))
        return jnp.repeat(jnp.exp(steps), dims[axis_at] // blocks).reshape((-1,) + (1,) * (len(dims) - axis_at - 1))

    level = one(*shards[0])
    for cut in shards[1:]:
        level = level * one(*cut)
    return level


def scatter_about(rng, shape, width, most, pieces=(), dtype=jnp.bfloat16):
    factor_of = shard_levels(rng, shape, pieces, -0.22, 0.18) if pieces else 1.0
    result = jax.random.normal(rng, shape, jnp.float32) * width * factor_of
    return jnp.minimum(jnp.maximum(result, -most), most).astype(dtype)


def setup_inputs(seed: int = 0) -> dict:
    keys = jax.random.split(jax.random.key(seed), 4)
    orbitals = scatter_about(keys[0], (NZ, NORB, NXY), 1.0, 6.0, ((0, 32), (1, 8)), jnp.float32)
    potential = jnp.clip(jax.random.uniform(keys[1], (NZ, NXY), jnp.float32, -4.0, 4.0) * shard_levels(keys[1], (NZ, NXY), ((0, 32),), -0.4, 0.0), -4.0, 4.0)
    projectors = scatter_about(keys[2], (NZ, NPROJ, NXY), (NX * NY * NZ // 64) ** -0.5, 0.09375, ((0, 32), (2, 8)), jnp.float32)
    return {"orbitals": orbitals, "potential": potential, "projectors": projectors}


grid_step = 0.5
center = 22.0
half_width = 18.0


def laplace(field):
    cube = field.reshape(field.shape[0], field.shape[1], NY, NX)
    total = -7.5 * cube
    for axis in (0, 2, 3):
        for offset, weight in ((1, 4.0 / 3.0), (2, -1.0 / 12.0)):
            total = total + weight * (jnp.roll(cube, offset, axis) + jnp.roll(cube, -offset, axis))
    return (total / (grid_step * grid_step)).reshape(field.shape)


def exchange_term(field, projectors):
    intersection = jnp.einsum("zpn,zon->po", projectors, field, precision=lax.Precision.HIGHEST)
    return -jnp.einsum("zpn,po->zon", projectors, intersection, precision=lax.Precision.HIGHEST)


def filter_step(field, potential, projectors):
    applied = -0.5 * laplace(field) + potential[:, None, :] * field + exchange_term(field, projectors)
    return (applied - center * field) / half_width


def reference(orbitals, potential, projectors):
    first = filter_step(orbitals, potential, projectors)
    return 2.0 * filter_step(first, potential, projectors) - orbitals
```

```python
import functools

import jax
import jax.numpy as jnp
from jax import lax
from jax.experimental import pallas as pl
from jax.experimental.pallas import tpu as pltpu
from jax.sharding import PartitionSpec as P

MESH = pl.DeviceIdType.MESH
F32 = jnp.float32
BF16 = jnp.bfloat16
CENTER = 22.0
SCALE = 2.0 / (18.0 * 18.0)
NEAR = -8.0 / 3.0
FAR = 1.0 / 6.0
NG = 32
NO = 8
ORB = 48
PROJ = 256
BLOCK = 512
TILES = 32
XTILES = 24


def lane_masks(rows):
    lane = lax.broadcasted_iota(jnp.int32, (rows, 128), 1)
    x = lax.rem(lane, 64)
    return lane < 64, x == 63, x == 0, x >= 62, x < 2


def stencil_tile(masks, here, before, after, z_near, z_far, diagonal):
    low, last1, first1, last2, first2 = masks
    swapped = pltpu.roll(here, 64, 1)
    crossed = jnp.where(low, pltpu.roll(before, 64, 1), pltpu.roll(after, 64, 1))
    near = z_near + crossed + swapped
    near += pltpu.roll(jnp.where(last1, swapped, here), 1, 1)
    near += pltpu.roll(jnp.where(first1, swapped, here), 127, 1)
    far = z_far + before + after
    far += pltpu.roll(jnp.where(last2, swapped, here), 2, 1)
    far += pltpu.roll(jnp.where(first2, swapped, here), 126, 1)
    return diagonal * here + NEAR * near + FAR * far


def split(x):
    high = x.astype(BF16)
    return high, (x - high.astype(F32)).astype(BF16)


def dot3(a, b, contract):
    dims = (contract, ((), ()))
    (ah, al), (bh, bl) = a, b
    total = lax.dot_general(ah, bh, dims, preferred_element_type=F32)
    total += lax.dot_general(ah, bl, dims, preferred_element_type=F32)
    total += lax.dot_general(al, bh, dims, preferred_element_type=F32)
    return total


NT = ((1,), (1,))
NN = ((1,), (0,))


def kernel(
    v_hbm, pot_hbm, proj_hbm, out_ref,
    v, vlo, vhi, u, ulo, uhi, pot, pext, plo, phi, pq_h, pq_l, vdom,
    gpart, xsend, xrecv, part, grecv, full, xall, gfull, wsend, wrecv,
    local_sem, halo_s, halo_r, uhalo_s, uhalo_r, phalo_s, phalo_r,
    vs, vr, xs, xr, g1s, g1r, g2s, g2r, as_, ar, ws, wr,
):
    g = lax.axis_index("grid")
    o = lax.axis_index("orb")

    def gdev(k):
        return lax.rem(g + k + NG, NG)

    def odev(k):
        return lax.rem(o + k + NO, NO)

    def copy(src, dst, ss, rs, axis, peer):
        return pltpu.make_async_remote_copy(
            src_ref=src, dst_ref=dst, send_sem=ss, recv_sem=rs,
            device_id={axis: peer}, device_id_type=MESH,
        )

    own = pl.ds(pl.multiple_of(o * BLOCK, BLOCK), BLOCK)
    loads = [
        pltpu.make_async_copy(proj_hbm, pext.at[:, :, pl.ds(128, BLOCK)], local_sem.at[0]),
        pltpu.make_async_copy(v_hbm, v, local_sem.at[1]),
        pltpu.make_async_copy(pot_hbm, pot, local_sem.at[2]),
        pltpu.make_async_copy(v_hbm.at[:, :, own], vdom.at[0], local_sem.at[3]),
    ]
    for c in loads:
        c.start()

    barrier = pltpu.get_barrier_semaphore()

    @pl.loop(1, NO)
    def _(k):
        pl.semaphore_signal(barrier, inc=1, device_id={"orb": odev(k)}, device_id_type=MESH)

    @pl.loop(1, NG)
    def _(k):
        pl.semaphore_signal(barrier, inc=1, device_id={"grid": gdev(k)}, device_id_type=MESH)

    pl.semaphore_wait(barrier, NG + NO - 2)

    pcopies = [
        copy(proj_hbm, plo, phalo_s.at[0], phalo_r.at[0], "grid", gdev(1)),
        copy(proj_hbm, phi, phalo_s.at[1], phalo_r.at[1], "grid", gdev(-1)),
        copy(proj_hbm.at[:, :, pl.ds(BLOCK - 128, 128)], pext.at[:, :, pl.ds(0, 128)],
             phalo_s.at[2], phalo_r.at[2], "orb", odev(1)),
        copy(proj_hbm.at[:, :, pl.ds(0, 128)], pext.at[:, :, pl.ds(BLOCK + 128, 128)],
             phalo_s.at[3], phalo_r.at[3], "orb", odev(-1)),
    ]
    for c in pcopies:
        c.start()

    def vcopy(k):
        block = pl.ds(pl.multiple_of(odev(k) * BLOCK, BLOCK), BLOCK)
        return copy(v_hbm.at[:, :, block], vdom.at[k], vs.at[k], vr.at[k], "orb", odev(k))

    @pl.loop(1, NO)
    def _(k):
        vcopy(k).start()

    vhalos = [
        copy(v_hbm, vlo, halo_s.at[0], halo_r.at[0], "grid", gdev(1)),
        copy(v_hbm, vhi, halo_s.at[1], halo_r.at[1], "grid", gdev(-1)),
    ]
    for c in vhalos:
        c.start()

    for c in loads:
        c.wait()
    for c in pcopies:
        c.wait_recv()

    pmasks = lane_masks(32)

    @pl.loop(0, PROJ // 32)
    def _(r):
        rows = pl.ds(pl.multiple_of(r * 32, 32), 32)
        qrows = pl.ds(pl.multiple_of(r * 32 + PROJ, 32), 32)
        for t in range(4):
            at = pl.ds(128 * t, 128)
            mid = pl.ds(128 * (t + 1), 128)
            low0, low1 = plo[0, rows, at], plo[1, rows, at]
            high0, high1 = phi[0, rows, at], phi[1, rows, at]
            own0, own1 = pext[0, rows, mid], pext[1, rows, mid]
            zs = ((low1 + own1, low0 + high0), (own0 + high0, low1 + high1))
            for z, here in ((0, own0), (1, own1)):
                lanes = pl.ds(pl.multiple_of(o * BLOCK + 128 * t, 128), 128)
                diagonal = pot[pl.ds(z, 1), lanes] + (15.0 - CENTER)
                q = stencil_tile(
                    pmasks, here, pext[z, rows, pl.ds(128 * t, 128)],
                    pext[z, rows, pl.ds(128 * (t + 2), 128)], zs[z][0], zs[z][1], diagonal,
                )
                hh, hl = split(here)
                qh, ql = split(q)
                pq_h[z, rows, at] = hh
                pq_l[z, rows, at] = hl
                pq_h[z, qrows, at] = qh
                pq_l[z, qrows, at] = ql

    gpart[...] = dot3(
        (pq_h[0, 0:PROJ], pq_l[0, 0:PROJ]), (pq_h[0, 0:PROJ], pq_l[0, 0:PROJ]), NT
    ) + dot3((pq_h[1, 0:PROJ], pq_l[1, 0:PROJ]), (pq_h[1, 0:PROJ], pq_l[1, 0:PROJ]), NT)

    def xcopy(k):
        return copy(xsend.at[k], xrecv.at[k], xs.at[k], xr.at[k], "orb", odev(-k))

    @pl.loop(0, NO)
    def _(k):
        @pl.when(k > 0)
        def _():
            vcopy(k).wait_recv()

        total = dot3(split(vdom[k, 0]), (pq_h[0], pq_l[0]), NT)
        total += dot3(split(vdom[k, 1]), (pq_h[1], pq_l[1]), NT)
        for i in range(6):
            for j in range(4):
                xsend[k, i * 4 + j] = total[8 * i:8 * i + 8, 128 * j:128 * j + 128]
        rows = gpart[pl.ds(pl.multiple_of(odev(-k) * 32, 32), 32), :]
        for i in range(4):
            for j in range(2):
                xsend[k, XTILES + i * 2 + j] = rows[8 * i:8 * i + 8, 128 * j:128 * j + 128]

        @pl.when(k > 0)
        def _():
            xcopy(k).start()

    vmasks = lane_masks(24)

    def apply_planes(src, lo, hi, store):
        @pl.loop(0, 32)
        def _(t):
            at = pl.ds(pl.multiple_of(t * 128, 128), 128)
            before = pl.ds(pl.multiple_of(lax.rem(t + 31, 32) * 128, 128), 128)
            after = pl.ds(pl.multiple_of(lax.rem(t + 1, 32) * 128, 128), 128)
            for r in (0, 24):
                rows = pl.ds(r, 24)
                low0, low1 = lo[0, rows, at], lo[1, rows, at]
                high0, high1 = hi[0, rows, at], hi[1, rows, at]
                own0, own1 = src[0, rows, at], src[1, rows, at]
                zs = ((low1 + own1, low0 + high0), (own0 + high0, low1 + high1))
                for z, here in ((0, own0), (1, own1)):
                    diagonal = pot[pl.ds(z, 1), at] + (15.0 - CENTER)
                    store(z, rows, at, stencil_tile(
                        vmasks, here, src[z, rows, before], src[z, rows, after],
                        zs[z][0], zs[z][1], diagonal,
                    ))

    for c in vhalos:
        c.wait_recv()

    def store_u(z, rows, at, value):
        u[z, rows, at] = value

    apply_planes(v, vlo, vhi, store_u)
    uhalos = [
        copy(u, ulo, uhalo_s.at[0], uhalo_r.at[0], "grid", gdev(1)),
        copy(u, uhi, uhalo_s.at[1], uhalo_r.at[1], "grid", gdev(-1)),
    ]

    part[...] = xsend[0]

    @pl.loop(1, NO)
    def _(k):
        xcopy(k).wait_recv()
        part[...] += xrecv[k]

    def scatter(k):
        return copy(part.at[gdev(k)], grecv.at[k], g1s.at[k], g1r.at[k], "grid", gdev(k))

    @pl.loop(1, NG)
    def _(k):
        scatter(k).start()

    for c in uhalos:
        c.start()

    @pl.loop(1, NG)
    def _(k):
        scatter(k).wait_recv()

    total = part[g]
    for k in range(1, NG):
        total += grecv[k]
    full[g] = total

    def spread(k, source):
        return copy(full.at[source], full.at[source], g2s.at[k], g2r.at[k], "grid", gdev(k))

    @pl.loop(1, NG)
    def _(k):
        spread(k, g).start()

    @pl.loop(1, NG)
    def _(k):
        spread(k, gdev(-k)).wait_recv()

    def acopy(k):
        return copy(full, xall.at[k], as_.at[k], ar.at[k], "orb", odev(k))

    @pl.loop(1, NO)
    def _(k):
        acopy(k).start()

    xall[0] = full[...]

    def place_g(k):
        for i in range(4):
            for j in range(2):
                gfull[pl.ds(pl.multiple_of(odev(-k) * 32 + 8 * i, 8), 8), pl.ds(128 * j, 128)] = (
                    xall[k, XTILES + i * 2 + j])

    place_g(0)

    @pl.loop(1, NO)
    def _(k):
        acopy(k).wait_recv()
        place_g(k)

    def wcopy(k):
        return copy(wsend.at[k], wrecv.at[k], ws.at[k], wr.at[k], "orb", odev(-k))

    @pl.loop(0, NO)
    def _(step):
        k = lax.rem(step + 1, NO)
        x = jnp.concatenate(
            [jnp.concatenate([xall[k, i * 4 + j] for j in range(4)], axis=1) for i in range(6)],
            axis=0,
        )
        x1, x2 = x[:, :PROJ], x[:, PROJ:]
        x2 = x2 - dot3(split(x1), split(gfull[...]), NN)
        c = split(jnp.concatenate([x2, x1], axis=1))
        for z in range(2):
            wsend[k, z] = dot3(c, (pq_h[z], pq_l[z]), NN)

        @pl.when(k > 0)
        def _():
            wcopy(k).start()

    for c in uhalos:
        c.wait_recv()

    def store_out(z, rows, at, value):
        out_ref[z, rows, at] = SCALE * value - v[z, rows, at]

    apply_planes(u, ulo, uhi, store_out)

    @pl.loop(0, NO)
    def _(k):
        block = pl.ds(pl.multiple_of(odev(k) * BLOCK, BLOCK), BLOCK)

        @pl.when(k == 0)
        def _():
            for z in range(2):
                out_ref[z, :, block] -= SCALE * wsend[0, z]

        @pl.when(k > 0)
        def _():
            wcopy(k).wait_recv()
            for z in range(2):
                out_ref[z, :, block] -= SCALE * wrecv[k, z]

    for c in pcopies + vhalos + uhalos:
        c.wait_send()

    @pl.loop(1, NO)
    def _(k):
        vcopy(k).wait_send()
        xcopy(k).wait_send()
        acopy(k).wait_send()
        wcopy(k).wait_send()

    @pl.loop(1, NG)
    def _(k):
        scatter(k).wait_send()
        spread(k, g).wait_send()


def shards(orbitals, potential, projectors):
    vm = pltpu.VMEM
    dma = pltpu.SemaphoreType.DMA
    field = (2, ORB, NO * BLOCK)
    scratch = [
        vm(field, F32), vm(field, F32), vm(field, F32), vm(field, F32), vm(field, F32), vm(field, F32),
        vm((2, NO * BLOCK), F32),
        vm((2, PROJ, BLOCK + 256), F32), vm((2, PROJ, BLOCK), F32), vm((2, PROJ, BLOCK), F32),
        vm((2, 2 * PROJ, BLOCK), BF16), vm((2, 2 * PROJ, BLOCK), BF16),
        vm((NO, 2, ORB, BLOCK), F32),
        vm((PROJ, PROJ), F32),
        vm((NO, TILES, 8, 128), F32), vm((NO, TILES, 8, 128), F32), vm((TILES, 8, 128), F32),
        vm((NG, 8, 128), F32), vm((TILES, 8, 128), F32), vm((NO, TILES, 8, 128), F32),
        vm((PROJ, PROJ), F32),
        vm((NO, 2, ORB, BLOCK), F32), vm((NO, 2, ORB, BLOCK), F32),
        dma((4,)), dma((2,)), dma((2,)), dma((2,)), dma((2,)), dma((4,)), dma((4,)),
        dma((NO,)), dma((NO,)), dma((NO,)), dma((NO,)),
        dma((NG,)), dma((NG,)), dma((NG,)), dma((NG,)),
        dma((NO,)), dma((NO,)), dma((NO,)), dma((NO,)),
    ]
    return pl.pallas_call(
        kernel,
        out_shape=jax.ShapeDtypeStruct(field, F32),
        in_specs=[pl.BlockSpec(memory_space=pl.ANY)] * 3,
        out_specs=pl.BlockSpec(memory_space=pltpu.VMEM),
        scratch_shapes=scratch,
        compiler_params=pltpu.CompilerParams(
            collective_id=0, has_side_effects=True, vmem_limit_bytes=56 * 1024 * 1024
        ),
    )(orbitals, potential, projectors)


def solution(mesh):
    placed = (P("grid", "orb", None), P("grid", None), P("grid", None, "orb"))
    return jax.shard_map(
        shards, mesh=mesh, in_specs=placed, out_specs=P("grid", "orb", None), check_vma=False
    )
```

```python
import functools

import jax
import jax.numpy as jnp
from jax import lax
from jax.experimental import pallas as pl
from jax.experimental.pallas import tpu as pltpu
from jax.sharding import PartitionSpec as P

MESH = pl.DeviceIdType.MESH
F32 = jnp.float32
BF16 = jnp.bfloat16
CENTER = 22.0
SCALE = 2.0 / (18.0 * 18.0)
NEAR = -8.0 / 3.0
FAR = 1.0 / 6.0
NG = 32
NC = 16
NO = 8
ORB = 48
PROJ = 256
BLOCK = 512
HALF = 16
XTILES = 12


def lane_masks(rows):
    lane = lax.broadcasted_iota(jnp.int32, (rows, 128), 1)
    x = lax.rem(lane, 64)
    return lane < 64, x == 63, x == 0, x >= 62, x < 2


def stencil_tile(masks, here, before, after, z_near, z_far, diagonal):
    low, last1, first1, last2, first2 = masks
    swapped = pltpu.roll(here, 64, 1)
    crossed = jnp.where(low, pltpu.roll(before, 64, 1), pltpu.roll(after, 64, 1))
    near = z_near + crossed + swapped
    near += pltpu.roll(jnp.where(last1, swapped, here), 1, 1)
    near += pltpu.roll(jnp.where(first1, swapped, here), 127, 1)
    far = z_far + before + after
    far += pltpu.roll(jnp.where(last2, swapped, here), 2, 1)
    far += pltpu.roll(jnp.where(first2, swapped, here), 126, 1)
    return diagonal * here + NEAR * near + FAR * far


def split(x):
    high = x.astype(BF16)
    return high, (x - high.astype(F32)).astype(BF16)


def dot3(a, b, contract):
    dims = (contract, ((), ()))
    (ah, al), (bh, bl) = a, b
    total = lax.dot_general(ah, bh, dims, preferred_element_type=F32)
    total += lax.dot_general(ah, bl, dims, preferred_element_type=F32)
    total += lax.dot_general(al, bh, dims, preferred_element_type=F32)
    return total


NT = ((1,), (1,))
NN = ((1,), (0,))


def kernel(
    v_hbm, pot_hbm, proj_hbm, out_ref,
    v, vlo, vhi, u, ulo, uhi, pot, pext, plo, phi, pq_h, pq_l, vdom,
    gpart, xsend, xpair, xsum, xrecv, part, grecv, full, xall, gfull, wsend, wrecv,
    vrel, urel, local_sem, pside_s, pside_r, psem, vsem, usem,
    vs, vr, xs, xr, g1s, g1r, g2s, g2r, as_, ar, ws, wr, pair_s, pair_r, bs, br,
):
    g = lax.axis_index("grid")
    o = lax.axis_index("orb")

    chip, core = g // 2, lax.rem(g, 2)
    partner = g + 1 - 2 * core

    def gdev(k):
        return lax.rem(g + k + NG, NG)

    def odev(k):
        return lax.rem(o + k + NO, NO)

    def copy(src, dst, ss, rs, axis, peer):
        return pltpu.make_async_remote_copy(
            src_ref=src, dst_ref=dst, send_sem=ss, recv_sem=rs,
            device_id={axis: peer}, device_id_type=MESH,
        )

    place = lax.rem(g, NC)
    top, bottom = place == NC - 1, place == 0
    relay_up, relay_down = place == 2, place == NC - 3

    def halo(src, lo, hi, rel, sem):
        def near(i, up):
            return copy(
                src.at[i], (lo if up else hi).at[i], sem.at[0 if up else 1, i],
                sem.at[2 if up else 3, i], "grid", gdev(1 if up else -1))

        def hop(up):
            return copy(
                src.at[int(up)], rel, sem.at[4, 0], sem.at[4, 1], "grid", gdev(3 if up else -3))

        def last(up):
            return copy(
                rel, (lo if up else hi).at[int(up)], sem.at[5, 0],
                sem.at[2 if up else 3, int(up)], "grid", gdev(-2 if up else 2))

        def start():
            @pl.when(top)
            def _():
                hop(True).start()

            @pl.when(bottom)
            def _():
                hop(False).start()

            near(0, True).start()
            near(1, False).start()

            @pl.when(jnp.logical_not(top))
            def _():
                near(1, True).start()

            @pl.when(jnp.logical_not(bottom))
            def _():
                near(0, False).start()

        def forward():
            @pl.when(relay_up)
            def _():
                hop(True).wait_recv()
                last(True).start()

            @pl.when(relay_down)
            def _():
                hop(False).wait_recv()
                last(False).start()

        def wait():
            for i in range(2):
                near(i, True).wait_recv()
                near(i, False).wait_recv()

        def finish():
            @pl.when(top)
            def _():
                hop(True).wait_send()

            @pl.when(bottom)
            def _():
                hop(False).wait_send()

            @pl.when(relay_up)
            def _():
                last(True).wait_send()

            @pl.when(relay_down)
            def _():
                last(False).wait_send()

            near(0, True).wait_send()
            near(1, False).wait_send()

            @pl.when(jnp.logical_not(top))
            def _():
                near(1, True).wait_send()

            @pl.when(jnp.logical_not(bottom))
            def _():
                near(0, False).wait_send()

        return start, forward, wait, finish

    own = pl.ds(pl.multiple_of(o * BLOCK, BLOCK), BLOCK)
    loads = [
        pltpu.make_async_copy(proj_hbm, pext.at[:, :, pl.ds(128, BLOCK)], local_sem.at[0]),
        pltpu.make_async_copy(v_hbm, v, local_sem.at[1]),
        pltpu.make_async_copy(pot_hbm, pot, local_sem.at[2]),
        pltpu.make_async_copy(v_hbm.at[:, :, own], vdom.at[0], local_sem.at[3]),
    ]
    for c in loads:
        c.start()

    barrier = pltpu.get_barrier_semaphore()

    @pl.loop(1, NO)
    def _(k):
        pl.semaphore_signal(barrier, inc=1, device_id={"orb": odev(k)}, device_id_type=MESH)

    @pl.loop(1, NC)
    def _(k):
        pl.semaphore_signal(barrier, inc=1, device_id={"grid": gdev(2 * k)}, device_id_type=MESH)

    for k in (1, -1, 3, -3):
        pl.semaphore_signal(barrier, inc=1, device_id={"grid": gdev(k)}, device_id_type=MESH)

    pl.semaphore_wait(barrier, NC + NO + 2)

    phalos = [
        copy(proj_hbm, plo, psem.at[0], psem.at[2], "grid", gdev(1)),
        copy(proj_hbm, phi, psem.at[1], psem.at[3], "grid", gdev(-1)),
    ]
    v_start, v_forward, v_wait, v_finish = halo(v_hbm, vlo, vhi, vrel, vsem)
    u_start, u_forward, u_wait, u_finish = halo(u, ulo, uhi, urel, usem)
    pcopies = [
        copy(proj_hbm.at[:, :, pl.ds(BLOCK - 128, 128)], pext.at[:, :, pl.ds(0, 128)],
             pside_s.at[0], pside_r.at[0], "orb", odev(1)),
        copy(proj_hbm.at[:, :, pl.ds(0, 128)], pext.at[:, :, pl.ds(BLOCK + 128, 128)],
             pside_s.at[1], pside_r.at[1], "orb", odev(-1)),
    ]
    for c in (*phalos, *pcopies):
        c.start()

    def vcopy(k):
        block = pl.ds(pl.multiple_of(odev(k) * BLOCK, BLOCK), BLOCK)
        return copy(v_hbm.at[:, :, block], vdom.at[k], vs.at[k], vr.at[k], "orb", odev(k))

    @pl.loop(1, NO)
    def _(k):
        vcopy(k).start()

    v_start()
    for c in loads:
        c.wait()
    for c in (*phalos, *pcopies):
        c.wait_recv()

    pmasks = lane_masks(32)

    @pl.loop(0, PROJ // 32)
    def _(r):
        rows = pl.ds(pl.multiple_of(r * 32, 32), 32)
        qrows = pl.ds(pl.multiple_of(r * 32 + PROJ, 32), 32)
        for t in range(4):
            at = pl.ds(128 * t, 128)
            mid = pl.ds(128 * (t + 1), 128)
            low0, low1 = plo[0, rows, at], plo[1, rows, at]
            high0, high1 = phi[0, rows, at], phi[1, rows, at]
            own0, own1 = pext[0, rows, mid], pext[1, rows, mid]
            zs = ((low1 + own1, low0 + high0), (own0 + high0, low1 + high1))
            for z, here in ((0, own0), (1, own1)):
                lanes = pl.ds(pl.multiple_of(o * BLOCK + 128 * t, 128), 128)
                diagonal = pot[pl.ds(z, 1), lanes] + (15.0 - CENTER)
                q = stencil_tile(
                    pmasks, here, pext[z, rows, pl.ds(128 * t, 128)],
                    pext[z, rows, pl.ds(128 * (t + 2), 128)], zs[z][0], zs[z][1], diagonal,
                )
                hh, hl = split(here)
                qh, ql = split(q)
                pq_h[z, rows, at] = hh
                pq_l[z, rows, at] = hl
                pq_h[z, qrows, at] = qh
                pq_l[z, qrows, at] = ql

    gpart[...] = dot3(
        (pq_h[0, 0:PROJ], pq_l[0, 0:PROJ]), (pq_h[0, 0:PROJ], pq_l[0, 0:PROJ]), NT
    ) + dot3((pq_h[1, 0:PROJ], pq_l[1, 0:PROJ]), (pq_h[1, 0:PROJ], pq_l[1, 0:PROJ]), NT)

    def pair(first):
        return copy(
            xsend.at[pl.ds(first, half), 1 - core], xpair.at[pl.ds(first, half)],
            pair_s.at[first // half], pair_r.at[first // half], "grid", partner,
        )

    def xcopy(k):
        return copy(xsum.at[k], xrecv.at[k], xs.at[k], xr.at[k], "orb", odev(-k))

    half = NO // 2
    for first in (0, half):
        for k in range(max(first, 1), first + half):
            vcopy(k).wait_recv()
        total = sum(
            dot3(
                split(vdom[first:first + half, z].reshape(half * ORB, BLOCK)),
                (pq_h[z], pq_l[z]), NT,
            )
            for z in range(2)
        )
        for n in range(half):
            k = first + n
            for i in range(6):
                for j in range(4):
                    row = ORB * n + 8 * i
                    t = i * 4 + j
                    xsend[k, t // XTILES, t % XTILES] = total[row:row + 8, 128 * j:128 * j + 128]
            rows = gpart[pl.ds(pl.multiple_of(odev(-k) * 32, 32), 32), :]
            for i in range(4):
                for j in range(2):
                    t = i * 2 + j
                    xsend[k, t // 4, XTILES + t % 4] = rows[8 * i:8 * i + 8, 128 * j:128 * j + 128]
        pair(first).start()

    vmasks = lane_masks(24)

    def apply_planes(src, lo, hi, store):
        @pl.loop(0, 32)
        def _(t):
            at = pl.ds(pl.multiple_of(t * 128, 128), 128)
            before = pl.ds(pl.multiple_of(lax.rem(t + 31, 32) * 128, 128), 128)
            after = pl.ds(pl.multiple_of(lax.rem(t + 1, 32) * 128, 128), 128)
            for r in (0, 24):
                rows = pl.ds(r, 24)
                low0, low1 = lo[0, rows, at], lo[1, rows, at]
                high0, high1 = hi[0, rows, at], hi[1, rows, at]
                own0, own1 = src[0, rows, at], src[1, rows, at]
                zs = ((low1 + own1, low0 + high0), (own0 + high0, low1 + high1))
                for z, here in ((0, own0), (1, own1)):
                    diagonal = pot[pl.ds(z, 1), at] + (15.0 - CENTER)
                    store(z, rows, at, stencil_tile(
                        vmasks, here, src[z, rows, before], src[z, rows, after],
                        zs[z][0], zs[z][1], diagonal,
                    ))

    def store_u(z, rows, at, value):
        u[z, rows, at] = value

    v_forward()

    for first in (0, half):
        pair(first).wait_recv()
        for k in range(first, first + half):
            xsum[k] = xsend[k, core] + xpair[k]
            if k > 0:
                xcopy(k).start()

    part[...] = xsum[0]

    @pl.loop(1, NO)
    def _(k):
        xcopy(k).wait_recv()
        part[...] += xrecv[k]

    def cdev(k):
        return lax.rem(chip + k + NC, NC)

    def scatter(k):
        return copy(part.at[cdev(k)], grecv.at[k], g1s.at[k], g1r.at[k], "grid", gdev(2 * k))

    @pl.loop(1, NC)
    def _(k):
        scatter(k).start()

    @pl.loop(1, NC)
    def _(k):
        scatter(k).wait_recv()

    total = part[chip]
    for k in range(1, NC):
        total += grecv[k]
    full[chip] = total

    def spread(k, source):
        return copy(full.at[source], full.at[source], g2s.at[k], g2r.at[k], "grid", gdev(2 * k))

    @pl.loop(1, NC)
    def _(k):
        spread(k, chip).start()

    v_wait()
    apply_planes(v, vlo, vhi, store_u)
    u_start()

    @pl.loop(1, NC)
    def _(k):
        spread(k, cdev(-k)).wait_recv()

    def acopy(k):
        return copy(full, xall.at[k, core], as_.at[k], ar.at[k], "orb", odev(k))

    def share(k):
        return copy(xall.at[k, core], xall.at[k, core], bs.at[k], br.at[k], "grid", partner)

    def shared(k):
        return copy(xall.at[k, core], xall.at[k, 1 - core], bs.at[k], br.at[k], "grid", partner)

    @pl.loop(1, NO)
    def _(k):
        acopy(k).start()

    u_forward()
    xall[0, core] = full[...]
    share(0).start()

    @pl.loop(1, NO)
    def _(k):
        acopy(k).wait_recv()
        share(k).start()

    @pl.loop(0, NO)
    def _(k):
        shared(k).wait_recv()
        for i in range(4):
            for j in range(2):
                t = i * 2 + j
                gfull[pl.ds(pl.multiple_of(odev(-k) * 32 + 8 * i, 8), 8), pl.ds(128 * j, 128)] = (
                    xall[k, t // 4, XTILES + t % 4])

    def wcopy(k):
        return copy(wsend.at[k], wrecv.at[k], ws.at[k], wr.at[k], "orb", odev(-k))

    gram = split(gfull[...])
    for first in (half, 0):
        x = jnp.concatenate(
            [
                jnp.concatenate(
                    [xall[k, (4 * i + j) // XTILES, (4 * i + j) % XTILES] for j in range(4)], axis=1)
                for k in range(first, first + half)
                for i in range(6)
            ],
            axis=0,
        )
        x1, x2 = x[:, :PROJ], x[:, PROJ:]
        x2 = x2 - dot3(split(x1), gram, NN)
        c = split(jnp.concatenate([x2, x1], axis=1))
        for z in range(2):
            wsend[first:first + half, z] = dot3(c, (pq_h[z], pq_l[z]), NN).reshape(half, ORB, BLOCK)
        for k in range(max(first, 1), first + half):
            wcopy(k).start()

    u_wait()

    def store_out(z, rows, at, value):
        out_ref[z, rows, at] = SCALE * value - v[z, rows, at]

    apply_planes(u, ulo, uhi, store_out)

    @pl.loop(0, NO)
    def _(k):
        block = pl.ds(pl.multiple_of(odev(k) * BLOCK, BLOCK), BLOCK)

        @pl.when(k == 0)
        def _():
            for z in range(2):
                out_ref[z, :, block] -= SCALE * wsend[0, z]

        @pl.when(k > 0)
        def _():
            wcopy(k).wait_recv()
            for z in range(2):
                out_ref[z, :, block] -= SCALE * wrecv[k, z]

    v_finish()
    u_finish()
    for c in (*phalos, *pcopies):
        c.wait_send()

    @pl.loop(1, NO)
    def _(k):
        vcopy(k).wait_send()
        xcopy(k).wait_send()
        acopy(k).wait_send()
        wcopy(k).wait_send()

    @pl.loop(1, NC)
    def _(k):
        scatter(k).wait_send()
        spread(k, chip).wait_send()

    @pl.loop(0, NO)
    def _(k):
        share(k).wait_send()

    for first in (0, half):
        pair(first).wait_send()


def shards(orbitals, potential, projectors):
    vm = pltpu.VMEM
    dma = pltpu.SemaphoreType.DMA
    field = (2, ORB, NO * BLOCK)
    scratch = [
        vm(field, F32), vm(field, F32), vm(field, F32), vm(field, F32), vm(field, F32), vm(field, F32),
        vm((2, NO * BLOCK), F32),
        vm((2, PROJ, BLOCK + 256), F32), vm((2, PROJ, BLOCK), F32), vm((2, PROJ, BLOCK), F32),
        vm((2, 2 * PROJ, BLOCK), BF16), vm((2, 2 * PROJ, BLOCK), BF16),
        vm((NO, 2, ORB, BLOCK), F32),
        vm((PROJ, PROJ), F32),
        vm((NO, 2, HALF, 8, 128), F32), vm((NO, HALF, 8, 128), F32), vm((NO, HALF, 8, 128), F32),
        vm((NO, HALF, 8, 128), F32), vm((HALF, 8, 128), F32),
        vm((NC, 8, 128), F32), vm((HALF, 8, 128), F32), vm((NO, 2, HALF, 8, 128), F32),
        vm((PROJ, PROJ), F32),
        vm((NO, 2, ORB, BLOCK), F32), vm((NO, 2, ORB, BLOCK), F32),
        vm((ORB, NO * BLOCK), F32), vm((ORB, NO * BLOCK), F32),
        dma((4,)), dma((2,)), dma((2,)), dma((4,)), dma((6, 2)), dma((6, 2)),
        dma((NO,)), dma((NO,)), dma((NO,)), dma((NO,)),
        dma((NC,)), dma((NC,)), dma((NC,)), dma((NC,)),
        dma((NO,)), dma((NO,)), dma((NO,)), dma((NO,)), dma((2,)), dma((2,)), dma((NO,)), dma((NO,)),
    ]
    return pl.pallas_call(
        kernel,
        out_shape=jax.ShapeDtypeStruct(field, F32),
        in_specs=[pl.BlockSpec(memory_space=pl.ANY)] * 3,
        out_specs=pl.BlockSpec(memory_space=pltpu.VMEM),
        scratch_shapes=scratch,
        compiler_params=pltpu.CompilerParams(
            collective_id=0, has_side_effects=True, vmem_limit_bytes=56 * 1024 * 1024
        ),
    )(orbitals, potential, projectors)


def solution(mesh):
    placed = (P("grid", "orb", None), P("grid", None), P("grid", None, "orb"))
    return jax.shard_map(
        shards, mesh=mesh, in_specs=placed, out_specs=P("grid", "orb", None), check_vma=False
    )
```

```python
import functools

import jax
import jax.numpy as jnp
from jax import lax
from jax.experimental import pallas as pl
from jax.experimental.pallas import tpu as pltpu
from jax.sharding import PartitionSpec as P

MESH = pl.DeviceIdType.MESH
F32 = jnp.float32
BF16 = jnp.bfloat16
CENTER = 22.0
SCALE = 2.0 / (18.0 * 18.0)
NEAR = -8.0 / 3.0
FAR = 1.0 / 6.0
NG = 32
NC = 16
NO = 8
ORB = 48
PROJ = 256
BLOCK = 512
HALF = 16
XTILES = 12


def lane_masks(rows):
    lane = lax.broadcasted_iota(jnp.int32, (rows, 128), 1)
    x = lax.rem(lane, 64)
    return lane < 64, x == 63, x == 0, x >= 62, x < 2


def stencil_tile(masks, here, before, after, z_near, z_far, diagonal):
    low, last1, first1, last2, first2 = masks
    swapped = pltpu.roll(here, 64, 1)
    crossed = jnp.where(low, pltpu.roll(before, 64, 1), pltpu.roll(after, 64, 1))
    near = z_near + crossed + swapped
    near += pltpu.roll(jnp.where(last1, swapped, here), 1, 1)
    near += pltpu.roll(jnp.where(first1, swapped, here), 127, 1)
    far = z_far + before + after
    far += pltpu.roll(jnp.where(last2, swapped, here), 2, 1)
    far += pltpu.roll(jnp.where(first2, swapped, here), 126, 1)
    return diagonal * here + NEAR * near + FAR * far


def split(x):
    high = x.astype(BF16)
    return high, (x - high.astype(F32)).astype(BF16)


def dot3(a, b, contract):
    dims = (contract, ((), ()))
    (ah, al), (bh, bl) = a, b
    total = lax.dot_general(ah, bh, dims, preferred_element_type=F32)
    total += lax.dot_general(ah, bl, dims, preferred_element_type=F32)
    total += lax.dot_general(al, bh, dims, preferred_element_type=F32)
    return total


NT = ((1,), (1,))
NN = ((1,), (0,))


def kernel(
    v_hbm, pot_hbm, proj_hbm, out_ref,
    v, vlo, vhi, u, ulo, uhi, pot, pext, plo, phi, pq_h, pq_l, vdom,
    gpart, xsend, xpair, xsum, xrecv, part, grecv, full, xall, gfull, wsend, wrecv,
    prel, vrel, urel, local_sem, pside_s, pside_r, psem, vsem, usem,
    vs, vr, xs, xr, g1s, g1r, g2s, g2r, as_, ar, ws, wr, pair_s, pair_r, bs, br,
):
    g = lax.axis_index("grid")
    o = lax.axis_index("orb")

    chip, core = g // 2, lax.rem(g, 2)
    partner = g + 1 - 2 * core

    def gdev(k):
        return lax.rem(g + k + NG, NG)

    def odev(k):
        return lax.rem(o + k + NO, NO)

    def copy(src, dst, ss, rs, axis, peer):
        return pltpu.make_async_remote_copy(
            src_ref=src, dst_ref=dst, send_sem=ss, recv_sem=rs,
            device_id={axis: peer}, device_id_type=MESH,
        )

    place = lax.rem(g, NC)
    top, bottom = place == NC - 1, place == 0
    relay_up, relay_down = place == 2, place == NC - 3

    def halo(src, lo, hi, rel, sem):
        def near(i, up):
            return copy(
                src.at[i], (lo if up else hi).at[i], sem.at[0 if up else 1, i],
                sem.at[2 if up else 3, i], "grid", gdev(1 if up else -1))

        def hop(up):
            return copy(
                src.at[int(up)], rel, sem.at[4, 0], sem.at[4, 1], "grid", gdev(3 if up else -3))

        def last(up):
            return copy(
                rel, (lo if up else hi).at[int(up)], sem.at[5, 0],
                sem.at[2 if up else 3, int(up)], "grid", gdev(-2 if up else 2))

        def start():
            @pl.when(top)
            def _():
                hop(True).start()

            @pl.when(bottom)
            def _():
                hop(False).start()

            near(0, True).start()
            near(1, False).start()

            @pl.when(jnp.logical_not(top))
            def _():
                near(1, True).start()

            @pl.when(jnp.logical_not(bottom))
            def _():
                near(0, False).start()

        def forward():
            @pl.when(relay_up)
            def _():
                hop(True).wait_recv()
                last(True).start()

            @pl.when(relay_down)
            def _():
                hop(False).wait_recv()
                last(False).start()

        def wait():
            for i in range(2):
                near(i, True).wait_recv()
                near(i, False).wait_recv()

        def finish():
            @pl.when(top)
            def _():
                hop(True).wait_send()

            @pl.when(bottom)
            def _():
                hop(False).wait_send()

            @pl.when(relay_up)
            def _():
                last(True).wait_send()

            @pl.when(relay_down)
            def _():
                last(False).wait_send()

            near(0, True).wait_send()
            near(1, False).wait_send()

            @pl.when(jnp.logical_not(top))
            def _():
                near(1, True).wait_send()

            @pl.when(jnp.logical_not(bottom))
            def _():
                near(0, False).wait_send()

        return start, forward, wait, finish

    own = pl.ds(pl.multiple_of(o * BLOCK, BLOCK), BLOCK)
    loads = [
        pltpu.make_async_copy(proj_hbm, pext.at[:, :, pl.ds(128, BLOCK)], local_sem.at[0]),
        pltpu.make_async_copy(v_hbm, v, local_sem.at[1]),
        pltpu.make_async_copy(pot_hbm, pot, local_sem.at[2]),
        pltpu.make_async_copy(v_hbm.at[:, :, own], vdom.at[0], local_sem.at[3]),
    ]
    for c in loads:
        c.start()

    barrier = pltpu.get_barrier_semaphore()

    @pl.loop(1, NO)
    def _(k):
        pl.semaphore_signal(barrier, inc=1, device_id={"orb": odev(k)}, device_id_type=MESH)

    @pl.loop(1, NC)
    def _(k):
        pl.semaphore_signal(barrier, inc=1, device_id={"grid": gdev(2 * k)}, device_id_type=MESH)

    for k in (1, -1, 3, -3):
        pl.semaphore_signal(barrier, inc=1, device_id={"grid": gdev(k)}, device_id_type=MESH)

    pl.semaphore_wait(barrier, NC + NO + 2)

    p_start, p_forward, p_wait, p_finish = halo(proj_hbm, plo, phi, prel, psem)
    v_start, v_forward, v_wait, v_finish = halo(v_hbm, vlo, vhi, vrel, vsem)
    u_start, u_forward, u_wait, u_finish = halo(u, ulo, uhi, urel, usem)
    pcopies = [
        copy(proj_hbm.at[:, :, pl.ds(BLOCK - 128, 128)], pext.at[:, :, pl.ds(0, 128)],
             pside_s.at[0], pside_r.at[0], "orb", odev(1)),
        copy(proj_hbm.at[:, :, pl.ds(0, 128)], pext.at[:, :, pl.ds(BLOCK + 128, 128)],
             pside_s.at[1], pside_r.at[1], "orb", odev(-1)),
    ]
    p_start()
    for c in pcopies:
        c.start()

    def vcopy(k):
        block = pl.ds(pl.multiple_of(odev(k) * BLOCK, BLOCK), BLOCK)
        return copy(v_hbm.at[:, :, block], vdom.at[k], vs.at[k], vr.at[k], "orb", odev(k))

    @pl.loop(1, NO)
    def _(k):
        vcopy(k).start()

    for c in loads:
        c.wait()
    p_forward()
    for c in pcopies:
        c.wait_recv()
    p_wait()
    v_start()

    pmasks = lane_masks(32)

    @pl.loop(0, PROJ // 32)
    def _(r):
        rows = pl.ds(pl.multiple_of(r * 32, 32), 32)
        qrows = pl.ds(pl.multiple_of(r * 32 + PROJ, 32), 32)
        for t in range(4):
            at = pl.ds(128 * t, 128)
            mid = pl.ds(128 * (t + 1), 128)
            low0, low1 = plo[0, rows, at], plo[1, rows, at]
            high0, high1 = phi[0, rows, at], phi[1, rows, at]
            own0, own1 = pext[0, rows, mid], pext[1, rows, mid]
            zs = ((low1 + own1, low0 + high0), (own0 + high0, low1 + high1))
            for z, here in ((0, own0), (1, own1)):
                lanes = pl.ds(pl.multiple_of(o * BLOCK + 128 * t, 128), 128)
                diagonal = pot[pl.ds(z, 1), lanes] + (15.0 - CENTER)
                q = stencil_tile(
                    pmasks, here, pext[z, rows, pl.ds(128 * t, 128)],
                    pext[z, rows, pl.ds(128 * (t + 2), 128)], zs[z][0], zs[z][1], diagonal,
                )
                hh, hl = split(here)
                qh, ql = split(q)
                pq_h[z, rows, at] = hh
                pq_l[z, rows, at] = hl
                pq_h[z, qrows, at] = qh
                pq_l[z, qrows, at] = ql

    gpart[...] = dot3(
        (pq_h[0, 0:PROJ], pq_l[0, 0:PROJ]), (pq_h[0, 0:PROJ], pq_l[0, 0:PROJ]), NT
    ) + dot3((pq_h[1, 0:PROJ], pq_l[1, 0:PROJ]), (pq_h[1, 0:PROJ], pq_l[1, 0:PROJ]), NT)

    def pair(first):
        return copy(
            xsend.at[pl.ds(first, half), 1 - core], xpair.at[pl.ds(first, half)],
            pair_s.at[first // half], pair_r.at[first // half], "grid", partner,
        )

    def xcopy(k):
        return copy(xsum.at[k], xrecv.at[k], xs.at[k], xr.at[k], "orb", odev(-k))

    half = NO // 2
    for first in (0, half):
        for k in range(max(first, 1), first + half):
            vcopy(k).wait_recv()
        total = sum(
            dot3(
                split(vdom[first:first + half, z].reshape(half * ORB, BLOCK)),
                (pq_h[z], pq_l[z]), NT,
            )
            for z in range(2)
        )
        for n in range(half):
            k = first + n
            for i in range(6):
                for j in range(4):
                    row = ORB * n + 8 * i
                    t = i * 4 + j
                    xsend[k, t // XTILES, t % XTILES] = total[row:row + 8, 128 * j:128 * j + 128]
            rows = gpart[pl.ds(pl.multiple_of(odev(-k) * 32, 32), 32), :]
            for i in range(4):
                for j in range(2):
                    t = i * 2 + j
                    xsend[k, t // 4, XTILES + t % 4] = rows[8 * i:8 * i + 8, 128 * j:128 * j + 128]
        pair(first).start()

    vmasks = lane_masks(24)

    def apply_planes(src, lo, hi, store):
        @pl.loop(0, 32)
        def _(t):
            at = pl.ds(pl.multiple_of(t * 128, 128), 128)
            before = pl.ds(pl.multiple_of(lax.rem(t + 31, 32) * 128, 128), 128)
            after = pl.ds(pl.multiple_of(lax.rem(t + 1, 32) * 128, 128), 128)
            for r in (0, 24):
                rows = pl.ds(r, 24)
                low0, low1 = lo[0, rows, at], lo[1, rows, at]
                high0, high1 = hi[0, rows, at], hi[1, rows, at]
                own0, own1 = src[0, rows, at], src[1, rows, at]
                zs = ((low1 + own1, low0 + high0), (own0 + high0, low1 + high1))
                for z, here in ((0, own0), (1, own1)):
                    diagonal = pot[pl.ds(z, 1), at] + (15.0 - CENTER)
                    store(z, rows, at, stencil_tile(
                        vmasks, here, src[z, rows, before], src[z, rows, after],
                        zs[z][0], zs[z][1], diagonal,
                    ))

    def store_u(z, rows, at, value):
        u[z, rows, at] = value

    v_forward()

    for first in (0, half):
        pair(first).wait_recv()
        for k in range(first, first + half):
            xsum[k] = xsend[k, core] + xpair[k]
            if k > 0:
                xcopy(k).start()

    part[...] = xsum[0]

    @pl.loop(1, NO)
    def _(k):
        xcopy(k).wait_recv()
        part[...] += xrecv[k]

    def cdev(k):
        return lax.rem(chip + k + NC, NC)

    def scatter(k):
        return copy(part.at[cdev(k)], grecv.at[k], g1s.at[k], g1r.at[k], "grid", gdev(2 * k))

    @pl.loop(1, NC)
    def _(k):
        scatter(k).start()

    @pl.loop(1, NC)
    def _(k):
        scatter(k).wait_recv()

    total = part[chip]
    for k in range(1, NC):
        total += grecv[k]
    full[chip] = total

    def spread(k, source):
        return copy(full.at[source], full.at[source], g2s.at[k], g2r.at[k], "grid", gdev(2 * k))

    @pl.loop(1, NC)
    def _(k):
        spread(k, chip).start()

    v_wait()
    apply_planes(v, vlo, vhi, store_u)
    u_start()

    @pl.loop(1, NC)
    def _(k):
        spread(k, cdev(-k)).wait_recv()

    def acopy(k):
        return copy(full, xall.at[k, core], as_.at[k], ar.at[k], "orb", odev(k))

    def share(k):
        return copy(xall.at[k, core], xall.at[k, core], bs.at[k], br.at[k], "grid", partner)

    def shared(k):
        return copy(xall.at[k, core], xall.at[k, 1 - core], bs.at[k], br.at[k], "grid", partner)

    @pl.loop(1, NO)
    def _(k):
        acopy(k).start()

    u_forward()
    xall[0, core] = full[...]
    share(0).start()

    @pl.loop(1, NO)
    def _(k):
        acopy(k).wait_recv()
        share(k).start()

    @pl.loop(0, NO)
    def _(k):
        shared(k).wait_recv()
        for i in range(4):
            for j in range(2):
                t = i * 2 + j
                gfull[pl.ds(pl.multiple_of(odev(-k) * 32 + 8 * i, 8), 8), pl.ds(128 * j, 128)] = (
                    xall[k, t // 4, XTILES + t % 4])

    def wcopy(k):
        return copy(wsend.at[k], wrecv.at[k], ws.at[k], wr.at[k], "orb", odev(-k))

    gram = split(gfull[...])
    for first in (half, 0):
        x = jnp.concatenate(
            [
                jnp.concatenate(
                    [xall[k, (4 * i + j) // XTILES, (4 * i + j) % XTILES] for j in range(4)], axis=1)
                for k in range(first, first + half)
                for i in range(6)
            ],
            axis=0,
        )
        x1, x2 = x[:, :PROJ], x[:, PROJ:]
        x2 = x2 - dot3(split(x1), gram, NN)
        c = split(jnp.concatenate([x2, x1], axis=1))
        for z in range(2):
            wsend[first:first + half, z] = dot3(c, (pq_h[z], pq_l[z]), NN).reshape(half, ORB, BLOCK)
        for k in range(max(first, 1), first + half):
            wcopy(k).start()

    u_wait()

    def store_out(z, rows, at, value):
        out_ref[z, rows, at] = SCALE * value - v[z, rows, at]

    apply_planes(u, ulo, uhi, store_out)

    @pl.loop(0, NO)
    def _(k):
        block = pl.ds(pl.multiple_of(odev(k) * BLOCK, BLOCK), BLOCK)

        @pl.when(k == 0)
        def _():
            for z in range(2):
                out_ref[z, :, block] -= SCALE * wsend[0, z]

        @pl.when(k > 0)
        def _():
            wcopy(k).wait_recv()
            for z in range(2):
                out_ref[z, :, block] -= SCALE * wrecv[k, z]

    v_finish()
    u_finish()
    p_finish()
    for c in pcopies:
        c.wait_send()

    @pl.loop(1, NO)
    def _(k):
        vcopy(k).wait_send()
        xcopy(k).wait_send()
        acopy(k).wait_send()
        wcopy(k).wait_send()

    @pl.loop(1, NC)
    def _(k):
        scatter(k).wait_send()
        spread(k, chip).wait_send()

    @pl.loop(0, NO)
    def _(k):
        share(k).wait_send()

    for first in (0, half):
        pair(first).wait_send()


def shards(orbitals, potential, projectors):
    vm = pltpu.VMEM
    dma = pltpu.SemaphoreType.DMA
    field = (2, ORB, NO * BLOCK)
    scratch = [
        vm(field, F32), vm(field, F32), vm(field, F32), vm(field, F32), vm(field, F32), vm(field, F32),
        vm((2, NO * BLOCK), F32),
        vm((2, PROJ, BLOCK + 256), F32), vm((2, PROJ, BLOCK), F32), vm((2, PROJ, BLOCK), F32),
        vm((2, 2 * PROJ, BLOCK), BF16), vm((2, 2 * PROJ, BLOCK), BF16),
        vm((NO, 2, ORB, BLOCK), F32),
        vm((PROJ, PROJ), F32),
        vm((NO, 2, HALF, 8, 128), F32), vm((NO, HALF, 8, 128), F32), vm((NO, HALF, 8, 128), F32),
        vm((NO, HALF, 8, 128), F32), vm((HALF, 8, 128), F32),
        vm((NC, 8, 128), F32), vm((HALF, 8, 128), F32), vm((NO, 2, HALF, 8, 128), F32),
        vm((PROJ, PROJ), F32),
        vm((NO, 2, ORB, BLOCK), F32), vm((NO, 2, ORB, BLOCK), F32),
        vm((PROJ, BLOCK), F32), vm((ORB, NO * BLOCK), F32), vm((ORB, NO * BLOCK), F32),
        dma((4,)), dma((2,)), dma((2,)), dma((6, 2)), dma((6, 2)), dma((6, 2)),
        dma((NO,)), dma((NO,)), dma((NO,)), dma((NO,)),
        dma((NC,)), dma((NC,)), dma((NC,)), dma((NC,)),
        dma((NO,)), dma((NO,)), dma((NO,)), dma((NO,)), dma((2,)), dma((2,)), dma((NO,)), dma((NO,)),
    ]
    return pl.pallas_call(
        kernel,
        out_shape=jax.ShapeDtypeStruct(field, F32),
        in_specs=[pl.BlockSpec(memory_space=pl.ANY)] * 3,
        out_specs=pl.BlockSpec(memory_space=pltpu.VMEM),
        scratch_shapes=scratch,
        compiler_params=pltpu.CompilerParams(
            collective_id=0, has_side_effects=True, vmem_limit_bytes=56 * 1024 * 1024
        ),
    )(orbitals, potential, projectors)


def solution(mesh):
    placed = (P("grid", "orb", None), P("grid", None), P("grid", None, "orb"))
    return jax.shard_map(
        shards, mesh=mesh, in_specs=placed, out_specs=P("grid", "orb", None), check_vma=False
    )
```

```python
import functools

import jax
import jax.numpy as jnp
from jax import lax
from jax.experimental import pallas as pl
from jax.experimental.pallas import tpu as pltpu
from jax.sharding import PartitionSpec as P

MESH = pl.DeviceIdType.MESH
F32 = jnp.float32
BF16 = jnp.bfloat16
CENTER = 22.0
SCALE = 2.0 / (18.0 * 18.0)
NEAR = -8.0 / 3.0
FAR = 1.0 / 6.0
NG = 32
NC = 16
NO = 8
ORB = 48
PROJ = 256
BLOCK = 512
HALF = 16
XTILES = 12


def lane_masks(rows):
    lane = lax.broadcasted_iota(jnp.int32, (rows, 128), 1)
    x = lax.rem(lane, 64)
    return lane < 64, x == 63, x == 0, x >= 62, x < 2


def stencil_tile(masks, here, before, after, z_near, z_far, diagonal):
    low, last1, first1, last2, first2 = masks
    swapped = pltpu.roll(here, 64, 1)
    crossed = jnp.where(low, pltpu.roll(before, 64, 1), pltpu.roll(after, 64, 1))
    near = z_near + crossed + swapped
    near += pltpu.roll(jnp.where(last1, swapped, here), 1, 1)
    near += pltpu.roll(jnp.where(first1, swapped, here), 127, 1)
    far = z_far + before + after
    far += pltpu.roll(jnp.where(last2, swapped, here), 2, 1)
    far += pltpu.roll(jnp.where(first2, swapped, here), 126, 1)
    return diagonal * here + NEAR * near + FAR * far


def split(x):
    high = x.astype(BF16)
    return high, (x - high.astype(F32)).astype(BF16)


def dot3(a, b, contract):
    dims = (contract, ((), ()))
    (ah, al), (bh, bl) = a, b
    total = lax.dot_general(ah, bh, dims, preferred_element_type=F32)
    total += lax.dot_general(ah, bl, dims, preferred_element_type=F32)
    total += lax.dot_general(al, bh, dims, preferred_element_type=F32)
    return total


NT = ((1,), (1,))
NN = ((1,), (0,))


def kernel(
    v_hbm, pot_hbm, proj_hbm, out_ref,
    v, vlo, vhi, u, ulo, uhi, pot, pext, plo, phi, pq_h, pq_l, vdom,
    gpart, xsend, xpair, xsum, xrecv, part, grecv, full, xall, gfull, wsend, wrecv,
    prel, vrel, urel, local_sem, pside_s, pside_r, psem, vsem, usem,
    vs, vr, xs, xr, g1s, g1r, g2s, g2r, as_, ar, ws, wr, pair_s, pair_r, bs, br,
):
    g = lax.axis_index("grid")
    o = lax.axis_index("orb")

    chip, core = g // 2, lax.rem(g, 2)
    partner = g + 1 - 2 * core

    def gdev(k):
        return lax.rem(g + k + NG, NG)

    def odev(k):
        return lax.rem(o + k + NO, NO)

    def copy(src, dst, ss, rs, axis, peer):
        return pltpu.make_async_remote_copy(
            src_ref=src, dst_ref=dst, send_sem=ss, recv_sem=rs,
            device_id={axis: peer}, device_id_type=MESH,
        )

    place = lax.rem(g, NC)
    top, bottom = place == NC - 1, place == 0
    relay_up, relay_down = place == 2, place == NC - 3

    def halo(src, lo, hi, rel, sem):
        def near(i, up):
            return copy(
                src.at[i], (lo if up else hi).at[i], sem.at[0 if up else 1, i],
                sem.at[2 if up else 3, i], "grid", gdev(1 if up else -1))

        def hop(up):
            return copy(
                src.at[int(up)], rel, sem.at[4, 0], sem.at[4, 1], "grid", gdev(3 if up else -3))

        def last(up):
            return copy(
                rel, (lo if up else hi).at[int(up)], sem.at[5, 0],
                sem.at[2 if up else 3, int(up)], "grid", gdev(-2 if up else 2))

        def start():
            @pl.when(top)
            def _():
                hop(True).start()

            @pl.when(bottom)
            def _():
                hop(False).start()

            near(0, True).start()
            near(1, False).start()

            @pl.when(jnp.logical_not(top))
            def _():
                near(1, True).start()

            @pl.when(jnp.logical_not(bottom))
            def _():
                near(0, False).start()

        def forward():
            @pl.when(relay_up)
            def _():
                hop(True).wait_recv()
                last(True).start()

            @pl.when(relay_down)
            def _():
                hop(False).wait_recv()
                last(False).start()

        def wait():
            for i in range(2):
                near(i, True).wait_recv()
                near(i, False).wait_recv()

        def finish():
            @pl.when(top)
            def _():
                hop(True).wait_send()

            @pl.when(bottom)
            def _():
                hop(False).wait_send()

            @pl.when(relay_up)
            def _():
                last(True).wait_send()

            @pl.when(relay_down)
            def _():
                last(False).wait_send()

            near(0, True).wait_send()
            near(1, False).wait_send()

            @pl.when(jnp.logical_not(top))
            def _():
                near(1, True).wait_send()

            @pl.when(jnp.logical_not(bottom))
            def _():
                near(0, False).wait_send()

        return start, forward, wait, finish

    own = pl.ds(pl.multiple_of(o * BLOCK, BLOCK), BLOCK)
    loads = [
        pltpu.make_async_copy(proj_hbm, pext.at[:, :, pl.ds(128, BLOCK)], local_sem.at[0]),
        pltpu.make_async_copy(v_hbm, v, local_sem.at[1]),
        pltpu.make_async_copy(pot_hbm, pot, local_sem.at[2]),
        pltpu.make_async_copy(v_hbm.at[:, :, own], vdom.at[0], local_sem.at[3]),
    ]
    for c in loads:
        c.start()

    barrier = pltpu.get_barrier_semaphore()

    @pl.loop(1, NO)
    def _(k):
        pl.semaphore_signal(barrier, inc=1, device_id={"orb": odev(k)}, device_id_type=MESH)

    @pl.loop(1, NC)
    def _(k):
        pl.semaphore_signal(barrier, inc=1, device_id={"grid": gdev(2 * k)}, device_id_type=MESH)

    for k in (1, -1, 3, -3):
        pl.semaphore_signal(barrier, inc=1, device_id={"grid": gdev(k)}, device_id_type=MESH)

    pl.semaphore_wait(barrier, NC + NO + 2)

    p_start, p_forward, p_wait, p_finish = halo(proj_hbm, plo, phi, prel, psem)
    v_start, v_forward, v_wait, v_finish = halo(v_hbm, vlo, vhi, vrel, vsem)
    u_start, u_forward, u_wait, u_finish = halo(u, ulo, uhi, urel, usem)
    pcopies = [
        copy(proj_hbm.at[:, :, pl.ds(BLOCK - 128, 128)], pext.at[:, :, pl.ds(0, 128)],
             pside_s.at[0], pside_r.at[0], "orb", odev(1)),
        copy(proj_hbm.at[:, :, pl.ds(0, 128)], pext.at[:, :, pl.ds(BLOCK + 128, 128)],
             pside_s.at[1], pside_r.at[1], "orb", odev(-1)),
    ]
    p_start()
    for c in pcopies:
        c.start()

    def vcopy(k):
        block = pl.ds(pl.multiple_of(odev(k) * BLOCK, BLOCK), BLOCK)
        return copy(v_hbm.at[:, :, block], vdom.at[k], vs.at[k], vr.at[k], "orb", odev(k))

    for k in (4, 1, 7, 2, 6, 5, 3):
        vcopy(k).start()

    for c in loads:
        c.wait()
    p_forward()
    for c in pcopies:
        c.wait_recv()
    p_wait()
    v_start()

    pmasks = lane_masks(32)

    @pl.loop(0, PROJ // 32)
    def _(r):
        rows = pl.ds(pl.multiple_of(r * 32, 32), 32)
        qrows = pl.ds(pl.multiple_of(r * 32 + PROJ, 32), 32)
        for t in range(4):
            at = pl.ds(128 * t, 128)
            mid = pl.ds(128 * (t + 1), 128)
            low0, low1 = plo[0, rows, at], plo[1, rows, at]
            high0, high1 = phi[0, rows, at], phi[1, rows, at]
            own0, own1 = pext[0, rows, mid], pext[1, rows, mid]
            zs = ((low1 + own1, low0 + high0), (own0 + high0, low1 + high1))
            for z, here in ((0, own0), (1, own1)):
                lanes = pl.ds(pl.multiple_of(o * BLOCK + 128 * t, 128), 128)
                diagonal = pot[pl.ds(z, 1), lanes] + (15.0 - CENTER)
                q = stencil_tile(
                    pmasks, here, pext[z, rows, pl.ds(128 * t, 128)],
                    pext[z, rows, pl.ds(128 * (t + 2), 128)], zs[z][0], zs[z][1], diagonal,
                )
                hh, hl = split(here)
                qh, ql = split(q)
                pq_h[z, rows, at] = hh
                pq_l[z, rows, at] = hl
                pq_h[z, qrows, at] = qh
                pq_l[z, qrows, at] = ql

    gpart[...] = dot3(
        (pq_h[0, 0:PROJ], pq_l[0, 0:PROJ]), (pq_h[0, 0:PROJ], pq_l[0, 0:PROJ]), NT
    ) + dot3((pq_h[1, 0:PROJ], pq_l[1, 0:PROJ]), (pq_h[1, 0:PROJ], pq_l[1, 0:PROJ]), NT)

    def pair(first):
        return copy(
            xsend.at[pl.ds(first, half), 1 - core], xpair.at[pl.ds(first, half)],
            pair_s.at[first // half], pair_r.at[first // half], "grid", partner,
        )

    def xcopy(k):
        return copy(xsum.at[k], xrecv.at[k], xs.at[k], xr.at[k], "orb", odev(-k))

    half = NO // 2
    for first in (0, half):
        for k in range(max(first, 1), first + half):
            vcopy(k).wait_recv()
        total = sum(
            dot3(
                split(vdom[first:first + half, z].reshape(half * ORB, BLOCK)),
                (pq_h[z], pq_l[z]), NT,
            )
            for z in range(2)
        )
        for n in range(half):
            k = first + n
            for i in range(6):
                for j in range(4):
                    row = ORB * n + 8 * i
                    t = i * 4 + j
                    xsend[k, t // XTILES, t % XTILES] = total[row:row + 8, 128 * j:128 * j + 128]
            rows = gpart[pl.ds(pl.multiple_of(odev(-k) * 32, 32), 32), :]
            for i in range(4):
                for j in range(2):
                    t = i * 2 + j
                    xsend[k, t // 4, XTILES + t % 4] = rows[8 * i:8 * i + 8, 128 * j:128 * j + 128]
        pair(first).start()

    vmasks = lane_masks(24)

    def apply_planes(src, lo, hi, store):
        @pl.loop(0, 32)
        def _(t):
            at = pl.ds(pl.multiple_of(t * 128, 128), 128)
            before = pl.ds(pl.multiple_of(lax.rem(t + 31, 32) * 128, 128), 128)
            after = pl.ds(pl.multiple_of(lax.rem(t + 1, 32) * 128, 128), 128)
            for r in (0, 24):
                rows = pl.ds(r, 24)
                low0, low1 = lo[0, rows, at], lo[1, rows, at]
                high0, high1 = hi[0, rows, at], hi[1, rows, at]
                own0, own1 = src[0, rows, at], src[1, rows, at]
                zs = ((low1 + own1, low0 + high0), (own0 + high0, low1 + high1))
                for z, here in ((0, own0), (1, own1)):
                    diagonal = pot[pl.ds(z, 1), at] + (15.0 - CENTER)
                    store(z, rows, at, stencil_tile(
                        vmasks, here, src[z, rows, before], src[z, rows, after],
                        zs[z][0], zs[z][1], diagonal,
                    ))

    def store_u(z, rows, at, value):
        u[z, rows, at] = value

    v_forward()

    for first in (0, half):
        pair(first).wait_recv()
        for k in range(first, first + half):
            xsum[k] = xsend[k, core] + xpair[k]
            if k > 0:
                xcopy(k).start()

    part[...] = xsum[0]

    @pl.loop(1, NO)
    def _(k):
        xcopy(k).wait_recv()
        part[...] += xrecv[k]

    def cdev(k):
        return lax.rem(chip + k + NC, NC)

    def scatter(k):
        return copy(part.at[cdev(k)], grecv.at[k], g1s.at[k], g1r.at[k], "grid", gdev(2 * k))

    @pl.loop(1, NC)
    def _(k):
        scatter(k).start()

    @pl.loop(1, NC)
    def _(k):
        scatter(k).wait_recv()

    total = part[chip]
    for k in range(1, NC):
        total += grecv[k]
    full[chip] = total

    def spread(k, source):
        return copy(full.at[source], full.at[source], g2s.at[k], g2r.at[k], "grid", gdev(2 * k))

    @pl.loop(1, NC)
    def _(k):
        spread(k, chip).start()

    v_wait()
    apply_planes(v, vlo, vhi, store_u)
    u_start()

    @pl.loop(1, NC)
    def _(k):
        spread(k, cdev(-k)).wait_recv()

    def acopy(k):
        return copy(full, xall.at[k, core], as_.at[k], ar.at[k], "orb", odev(k))

    def share(k):
        return copy(xall.at[k, core], xall.at[k, core], bs.at[k], br.at[k], "grid", partner)

    def shared(k):
        return copy(xall.at[k, core], xall.at[k, 1 - core], bs.at[k], br.at[k], "grid", partner)

    @pl.loop(1, NO)
    def _(k):
        acopy(k).start()

    u_forward()
    xall[0, core] = full[...]
    share(0).start()

    @pl.loop(1, NO)
    def _(k):
        acopy(k).wait_recv()
        share(k).start()

    @pl.loop(0, NO)
    def _(k):
        shared(k).wait_recv()
        for i in range(4):
            for j in range(2):
                t = i * 2 + j
                gfull[pl.ds(pl.multiple_of(odev(-k) * 32 + 8 * i, 8), 8), pl.ds(128 * j, 128)] = (
                    xall[k, t // 4, XTILES + t % 4])

    def wcopy(k):
        return copy(wsend.at[k], wrecv.at[k], ws.at[k], wr.at[k], "orb", odev(-k))

    gram = split(gfull[...])
    for first in (half, 0):
        x = jnp.concatenate(
            [
                jnp.concatenate(
                    [xall[k, (4 * i + j) // XTILES, (4 * i + j) % XTILES] for j in range(4)], axis=1)
                for k in range(first, first + half)
                for i in range(6)
            ],
            axis=0,
        )
        x1, x2 = x[:, :PROJ], x[:, PROJ:]
        x2 = x2 - dot3(split(x1), gram, NN)
        c = split(jnp.concatenate([x2, x1], axis=1))
        for z in range(2):
            wsend[first:first + half, z] = dot3(c, (pq_h[z], pq_l[z]), NN).reshape(half, ORB, BLOCK)
        for k in range(max(first, 1), first + half):
            wcopy(k).start()

    u_wait()

    def store_out(z, rows, at, value):
        out_ref[z, rows, at] = SCALE * value - v[z, rows, at]

    apply_planes(u, ulo, uhi, store_out)

    @pl.loop(0, NO)
    def _(k):
        block = pl.ds(pl.multiple_of(odev(k) * BLOCK, BLOCK), BLOCK)

        @pl.when(k == 0)
        def _():
            for z in range(2):
                out_ref[z, :, block] -= SCALE * wsend[0, z]

        @pl.when(k > 0)
        def _():
            wcopy(k).wait_recv()
            for z in range(2):
                out_ref[z, :, block] -= SCALE * wrecv[k, z]

    v_finish()
    u_finish()
    p_finish()
    for c in pcopies:
        c.wait_send()

    @pl.loop(1, NO)
    def _(k):
        vcopy(k).wait_send()
        xcopy(k).wait_send()
        acopy(k).wait_send()
        wcopy(k).wait_send()

    @pl.loop(1, NC)
    def _(k):
        scatter(k).wait_send()
        spread(k, chip).wait_send()

    @pl.loop(0, NO)
    def _(k):
        share(k).wait_send()

    for first in (0, half):
        pair(first).wait_send()


def shards(orbitals, potential, projectors):
    vm = pltpu.VMEM
    dma = pltpu.SemaphoreType.DMA
    field = (2, ORB, NO * BLOCK)
    scratch = [
        vm(field, F32), vm(field, F32), vm(field, F32), vm(field, F32), vm(field, F32), vm(field, F32),
        vm((2, NO * BLOCK), F32),
        vm((2, PROJ, BLOCK + 256), F32), vm((2, PROJ, BLOCK), F32), vm((2, PROJ, BLOCK), F32),
        vm((2, 2 * PROJ, BLOCK), BF16), vm((2, 2 * PROJ, BLOCK), BF16),
        vm((NO, 2, ORB, BLOCK), F32),
        vm((PROJ, PROJ), F32),
        vm((NO, 2, HALF, 8, 128), F32), vm((NO, HALF, 8, 128), F32), vm((NO, HALF, 8, 128), F32),
        vm((NO, HALF, 8, 128), F32), vm((HALF, 8, 128), F32),
        vm((NC, 8, 128), F32), vm((HALF, 8, 128), F32), vm((NO, 2, HALF, 8, 128), F32),
        vm((PROJ, PROJ), F32),
        vm((NO, 2, ORB, BLOCK), F32), vm((NO, 2, ORB, BLOCK), F32),
        vm((PROJ, BLOCK), F32), vm((ORB, NO * BLOCK), F32), vm((ORB, NO * BLOCK), F32),
        dma((4,)), dma((2,)), dma((2,)), dma((6, 2)), dma((6, 2)), dma((6, 2)),
        dma((NO,)), dma((NO,)), dma((NO,)), dma((NO,)),
        dma((NC,)), dma((NC,)), dma((NC,)), dma((NC,)),
        dma((NO,)), dma((NO,)), dma((NO,)), dma((NO,)), dma((2,)), dma((2,)), dma((NO,)), dma((NO,)),
    ]
    return pl.pallas_call(
        kernel,
        out_shape=jax.ShapeDtypeStruct(field, F32),
        in_specs=[pl.BlockSpec(memory_space=pl.ANY)] * 3,
        out_specs=pl.BlockSpec(memory_space=pltpu.VMEM),
        scratch_shapes=scratch,
        compiler_params=pltpu.CompilerParams(
            collective_id=0, has_side_effects=True, vmem_limit_bytes=56 * 1024 * 1024
        ),
    )(orbitals, potential, projectors)


def solution(mesh):
    placed = (P("grid", "orb", None), P("grid", None), P("grid", None, "orb"))
    return jax.shard_map(
        shards, mesh=mesh, in_specs=placed, out_specs=P("grid", "orb", None), check_vma=False
    )
```

```python
import functools

import jax
import jax.numpy as jnp
from jax import lax
from jax.experimental import pallas as pl
from jax.experimental.pallas import tpu as pltpu
from jax.sharding import PartitionSpec as P

MESH = pl.DeviceIdType.MESH
F32 = jnp.float32
BF16 = jnp.bfloat16
CENTER = 22.0
SCALE = 2.0 / (18.0 * 18.0)
NEAR = -8.0 / 3.0
FAR = 1.0 / 6.0
NG = 32
NC = 16
NO = 8
ORB = 48
PROJ = 256
BLOCK = 512
HALF = 16
XTILES = 12


def lane_masks(rows):
    lane = lax.broadcasted_iota(jnp.int32, (rows, 128), 1)
    x = lax.rem(lane, 64)
    return lane < 64, x == 63, x == 0, x >= 62, x < 2


def stencil_tile(masks, here, before, after, z_near, z_far, diagonal):
    low, last1, first1, last2, first2 = masks
    swapped = pltpu.roll(here, 64, 1)
    crossed = jnp.where(low, pltpu.roll(before, 64, 1), pltpu.roll(after, 64, 1))
    near = z_near + crossed + swapped
    near += pltpu.roll(jnp.where(last1, swapped, here), 1, 1)
    near += pltpu.roll(jnp.where(first1, swapped, here), 127, 1)
    far = z_far + before + after
    far += pltpu.roll(jnp.where(last2, swapped, here), 2, 1)
    far += pltpu.roll(jnp.where(first2, swapped, here), 126, 1)
    return diagonal * here + NEAR * near + FAR * far


def split(x):
    high = x.astype(BF16)
    return high, (x - high.astype(F32)).astype(BF16)


def dot3(a, b, contract):
    dims = (contract, ((), ()))
    (ah, al), (bh, bl) = a, b
    total = lax.dot_general(ah, bh, dims, preferred_element_type=F32)
    total += lax.dot_general(ah, bl, dims, preferred_element_type=F32)
    total += lax.dot_general(al, bh, dims, preferred_element_type=F32)
    return total


NT = ((1,), (1,))
NN = ((1,), (0,))


def kernel(
    v_hbm, pot_hbm, proj_hbm, out_ref,
    v, vlo, vhi, u, ulo, uhi, pot, pext, plo, phi, pq_h, pq_l, vdom,
    gpart, xsend, xpair, xsum, xrecv, part, grecv, full, xall, gfull, wsend, wrecv,
    prel, vrel, urel, local_sem, pside_s, pside_r, psem, vsem, usem,
    vs, vr, xs, xr, g1s, g1r, g2s, g2r, as_, ar, ws, wr, pair_s, pair_r, bs, br,
):
    g = lax.axis_index("grid")
    o = lax.axis_index("orb")

    chip, core = g // 2, lax.rem(g, 2)
    partner = g + 1 - 2 * core

    def gdev(k):
        return lax.rem(g + k + NG, NG)

    def odev(k):
        return lax.rem(o + k + NO, NO)

    def copy(src, dst, ss, rs, axis, peer):
        return pltpu.make_async_remote_copy(
            src_ref=src, dst_ref=dst, send_sem=ss, recv_sem=rs,
            device_id={axis: peer}, device_id_type=MESH,
        )

    place = lax.rem(g, NC)
    top, bottom = place == NC - 1, place == 0
    relay_up, relay_down = place == 2, place == NC - 3

    def halo(src, lo, hi, rel, sem):
        def near(i, up):
            return copy(
                src.at[i], (lo if up else hi).at[i], sem.at[0 if up else 1, i],
                sem.at[2 if up else 3, i], "grid", gdev(1 if up else -1))

        def hop(up):
            return copy(
                src.at[int(up)], rel, sem.at[4, 0], sem.at[4, 1], "grid", gdev(3 if up else -3))

        def last(up):
            return copy(
                rel, (lo if up else hi).at[int(up)], sem.at[5, 0],
                sem.at[2 if up else 3, int(up)], "grid", gdev(-2 if up else 2))

        def start():
            @pl.when(top)
            def _():
                hop(True).start()

            @pl.when(bottom)
            def _():
                hop(False).start()

            near(0, True).start()
            near(1, False).start()

            @pl.when(jnp.logical_not(top))
            def _():
                near(1, True).start()

            @pl.when(jnp.logical_not(bottom))
            def _():
                near(0, False).start()

        def forward():
            @pl.when(relay_up)
            def _():
                hop(True).wait_recv()
                last(True).start()

            @pl.when(relay_down)
            def _():
                hop(False).wait_recv()
                last(False).start()

        def wait():
            for i in range(2):
                near(i, True).wait_recv()
                near(i, False).wait_recv()

        def finish():
            @pl.when(top)
            def _():
                hop(True).wait_send()

            @pl.when(bottom)
            def _():
                hop(False).wait_send()

            @pl.when(relay_up)
            def _():
                last(True).wait_send()

            @pl.when(relay_down)
            def _():
                last(False).wait_send()

            near(0, True).wait_send()
            near(1, False).wait_send()

            @pl.when(jnp.logical_not(top))
            def _():
                near(1, True).wait_send()

            @pl.when(jnp.logical_not(bottom))
            def _():
                near(0, False).wait_send()

        return start, forward, wait, finish

    own = pl.ds(pl.multiple_of(o * BLOCK, BLOCK), BLOCK)
    loads = [
        pltpu.make_async_copy(proj_hbm, pext.at[:, :, pl.ds(128, BLOCK)], local_sem.at[0]),
        pltpu.make_async_copy(v_hbm, v, local_sem.at[1]),
        pltpu.make_async_copy(pot_hbm, pot, local_sem.at[2]),
        pltpu.make_async_copy(v_hbm.at[:, :, own], vdom.at[0], local_sem.at[3]),
    ]
    for c in loads:
        c.start()

    barrier = pltpu.get_barrier_semaphore()

    @pl.loop(1, NO)
    def _(k):
        pl.semaphore_signal(barrier, inc=1, device_id={"orb": odev(k)}, device_id_type=MESH)

    @pl.loop(1, NC)
    def _(k):
        pl.semaphore_signal(barrier, inc=1, device_id={"grid": gdev(2 * k)}, device_id_type=MESH)

    for k in (1, -1, 3, -3):
        pl.semaphore_signal(barrier, inc=1, device_id={"grid": gdev(k)}, device_id_type=MESH)

    pl.semaphore_wait(barrier, NC + NO + 2)

    p_start, p_forward, p_wait, p_finish = halo(proj_hbm, plo, phi, prel, psem)
    v_start, v_forward, v_wait, v_finish = halo(v_hbm, vlo, vhi, vrel, vsem)
    u_start, u_forward, u_wait, u_finish = halo(u, ulo, uhi, urel, usem)
    pcopies = [
        copy(proj_hbm.at[:, :, pl.ds(BLOCK - 128, 128)], pext.at[:, :, pl.ds(0, 128)],
             pside_s.at[0], pside_r.at[0], "orb", odev(1)),
        copy(proj_hbm.at[:, :, pl.ds(0, 128)], pext.at[:, :, pl.ds(BLOCK + 128, 128)],
             pside_s.at[1], pside_r.at[1], "orb", odev(-1)),
    ]
    p_start()
    for c in pcopies:
        c.start()

    def vcopy(k):
        block = pl.ds(pl.multiple_of(odev(k) * BLOCK, BLOCK), BLOCK)
        return copy(v_hbm.at[:, :, block], vdom.at[k], vs.at[k], vr.at[k], "orb", odev(k))

    for k in (4, 1, 7, 2, 6, 5, 3):
        vcopy(k).start()

    for c in loads:
        c.wait()
    p_forward()
    for c in pcopies:
        c.wait_recv()
    p_wait()
    v_start()

    pmasks = lane_masks(32)

    @pl.loop(0, PROJ // 32)
    def _(r):
        rows = pl.ds(pl.multiple_of(r * 32, 32), 32)
        qrows = pl.ds(pl.multiple_of(r * 32 + PROJ, 32), 32)
        for t in range(4):
            at = pl.ds(128 * t, 128)
            mid = pl.ds(128 * (t + 1), 128)
            low0, low1 = plo[0, rows, at], plo[1, rows, at]
            high0, high1 = phi[0, rows, at], phi[1, rows, at]
            own0, own1 = pext[0, rows, mid], pext[1, rows, mid]
            zs = ((low1 + own1, low0 + high0), (own0 + high0, low1 + high1))
            for z, here in ((0, own0), (1, own1)):
                lanes = pl.ds(pl.multiple_of(o * BLOCK + 128 * t, 128), 128)
                diagonal = pot[pl.ds(z, 1), lanes] + (15.0 - CENTER)
                q = stencil_tile(
                    pmasks, here, pext[z, rows, pl.ds(128 * t, 128)],
                    pext[z, rows, pl.ds(128 * (t + 2), 128)], zs[z][0], zs[z][1], diagonal,
                )
                hh, hl = split(here)
                qh, ql = split(q)
                pq_h[z, rows, at] = hh
                pq_l[z, rows, at] = hl
                pq_h[z, qrows, at] = qh
                pq_l[z, qrows, at] = ql

    gpart[...] = dot3(
        (pq_h[0, 0:PROJ], pq_l[0, 0:PROJ]), (pq_h[0, 0:PROJ], pq_l[0, 0:PROJ]), NT
    ) + dot3((pq_h[1, 0:PROJ], pq_l[1, 0:PROJ]), (pq_h[1, 0:PROJ], pq_l[1, 0:PROJ]), NT)

    def pair(first):
        return copy(
            xsend.at[pl.ds(first, half), 1 - core], xpair.at[pl.ds(first, half)],
            pair_s.at[first // half], pair_r.at[first // half], "grid", partner,
        )

    def xcopy(k):
        return copy(xsum.at[k], xrecv.at[k], xs.at[k], xr.at[k], "orb", odev(-k))

    half = NO // 2
    for first in (0, half):
        for k in range(max(first, 1), first + half):
            vcopy(k).wait_recv()
        total = sum(
            dot3(
                split(vdom[first:first + half, z].reshape(half * ORB, BLOCK)),
                (pq_h[z], pq_l[z]), NT,
            )
            for z in range(2)
        )
        for n in range(half):
            k = first + n
            for i in range(6):
                for j in range(4):
                    row = ORB * n + 8 * i
                    t = i * 4 + j
                    xsend[k, t // XTILES, t % XTILES] = total[row:row + 8, 128 * j:128 * j + 128]
            rows = gpart[pl.ds(pl.multiple_of(odev(-k) * 32, 32), 32), :]
            for i in range(4):
                for j in range(2):
                    t = i * 2 + j
                    xsend[k, t // 4, XTILES + t % 4] = rows[8 * i:8 * i + 8, 128 * j:128 * j + 128]
        pair(first).start()

    vmasks = lane_masks(24)

    def apply_planes(src, lo, hi, store):
        @pl.loop(0, 32)
        def _(t):
            at = pl.ds(pl.multiple_of(t * 128, 128), 128)
            before = pl.ds(pl.multiple_of(lax.rem(t + 31, 32) * 128, 128), 128)
            after = pl.ds(pl.multiple_of(lax.rem(t + 1, 32) * 128, 128), 128)
            for r in (0, 24):
                rows = pl.ds(r, 24)
                low0, low1 = lo[0, rows, at], lo[1, rows, at]
                high0, high1 = hi[0, rows, at], hi[1, rows, at]
                own0, own1 = src[0, rows, at], src[1, rows, at]
                zs = ((low1 + own1, low0 + high0), (own0 + high0, low1 + high1))
                for z, here in ((0, own0), (1, own1)):
                    diagonal = pot[pl.ds(z, 1), at] + (15.0 - CENTER)
                    store(z, rows, at, stencil_tile(
                        vmasks, here, src[z, rows, before], src[z, rows, after],
                        zs[z][0], zs[z][1], diagonal,
                    ))

    def store_u(z, rows, at, value):
        u[z, rows, at] = value

    v_forward()

    for first in (0, half):
        pair(first).wait_recv()
        for k in range(first, first + half):
            xsum[k] = xsend[k, core] + xpair[k]
            if k > 0:
                xcopy(k).start()

    part[...] = xsum[0]

    @pl.loop(1, NO)
    def _(k):
        xcopy(k).wait_recv()
        part[...] += xrecv[k]

    def cdev(k):
        return lax.rem(chip + k + NC, NC)

    def scatter(k):
        return copy(part.at[cdev(k)], grecv.at[k], g1s.at[k], g1r.at[k], "grid", gdev(2 * k))

    @pl.loop(1, NC)
    def _(k):
        scatter(k).start()

    @pl.loop(1, NC)
    def _(k):
        scatter(k).wait_recv()

    total = part[chip]
    for k in range(1, NC):
        total += grecv[k]
    full[chip] = total

    def spread(k, source):
        return copy(full.at[source], full.at[source], g2s.at[k], g2r.at[k], "grid", gdev(2 * k))

    @pl.loop(1, NC)
    def _(k):
        spread(k, chip).start()

    v_wait()
    apply_planes(v, vlo, vhi, store_u)
    u_start()

    @pl.loop(1, NC)
    def _(k):
        spread(k, cdev(-k)).wait_recv()

    def acopy(k):
        return copy(full, xall.at[k, core], as_.at[k], ar.at[k], "orb", odev(k))

    def share(k):
        return copy(xall.at[k, core], xall.at[k, core], bs.at[k], br.at[k], "grid", partner)

    def shared(k):
        return copy(xall.at[k, core], xall.at[k, 1 - core], bs.at[k], br.at[k], "grid", partner)

    for k in (4, 1, 7, 2, 6, 5, 3):
        acopy(k).start()

    u_forward()
    xall[0, core] = full[...]
    share(0).start()

    @pl.loop(1, NO)
    def _(k):
        acopy(k).wait_recv()
        share(k).start()

    @pl.loop(0, NO)
    def _(k):
        shared(k).wait_recv()
        for i in range(4):
            for j in range(2):
                t = i * 2 + j
                gfull[pl.ds(pl.multiple_of(odev(-k) * 32 + 8 * i, 8), 8), pl.ds(128 * j, 128)] = (
                    xall[k, t // 4, XTILES + t % 4])

    def wcopy(k):
        return copy(wsend.at[k], wrecv.at[k], ws.at[k], wr.at[k], "orb", odev(-k))

    gram = split(gfull[...])
    for first in (half, 0):
        x = jnp.concatenate(
            [
                jnp.concatenate(
                    [xall[k, (4 * i + j) // XTILES, (4 * i + j) % XTILES] for j in range(4)], axis=1)
                for k in range(first, first + half)
                for i in range(6)
            ],
            axis=0,
        )
        x1, x2 = x[:, :PROJ], x[:, PROJ:]
        x2 = x2 - dot3(split(x1), gram, NN)
        c = split(jnp.concatenate([x2, x1], axis=1))
        for z in range(2):
            wsend[first:first + half, z] = dot3(c, (pq_h[z], pq_l[z]), NN).reshape(half, ORB, BLOCK)
        for k in (4, 7, 5, 6) if first else (1, 3, 2):
            wcopy(k).start()

    u_wait()

    def store_out(z, rows, at, value):
        out_ref[z, rows, at] = SCALE * value - v[z, rows, at]

    apply_planes(u, ulo, uhi, store_out)

    @pl.loop(0, NO)
    def _(k):
        block = pl.ds(pl.multiple_of(odev(k) * BLOCK, BLOCK), BLOCK)

        @pl.when(k == 0)
        def _():
            for z in range(2):
                out_ref[z, :, block] -= SCALE * wsend[0, z]

        @pl.when(k > 0)
        def _():
            wcopy(k).wait_recv()
            for z in range(2):
                out_ref[z, :, block] -= SCALE * wrecv[k, z]

    v_finish()
    u_finish()
    p_finish()
    for c in pcopies:
        c.wait_send()

    @pl.loop(1, NO)
    def _(k):
        vcopy(k).wait_send()
        xcopy(k).wait_send()
        acopy(k).wait_send()
        wcopy(k).wait_send()

    @pl.loop(1, NC)
    def _(k):
        scatter(k).wait_send()
        spread(k, chip).wait_send()

    @pl.loop(0, NO)
    def _(k):
        share(k).wait_send()

    for first in (0, half):
        pair(first).wait_send()


def shards(orbitals, potential, projectors):
    vm = pltpu.VMEM
    dma = pltpu.SemaphoreType.DMA
    field = (2, ORB, NO * BLOCK)
    scratch = [
        vm(field, F32), vm(field, F32), vm(field, F32), vm(field, F32), vm(field, F32), vm(field, F32),
        vm((2, NO * BLOCK), F32),
        vm((2, PROJ, BLOCK + 256), F32), vm((2, PROJ, BLOCK), F32), vm((2, PROJ, BLOCK), F32),
        vm((2, 2 * PROJ, BLOCK), BF16), vm((2, 2 * PROJ, BLOCK), BF16),
        vm((NO, 2, ORB, BLOCK), F32),
        vm((PROJ, PROJ), F32),
        vm((NO, 2, HALF, 8, 128), F32), vm((NO, HALF, 8, 128), F32), vm((NO, HALF, 8, 128), F32),
        vm((NO, HALF, 8, 128), F32), vm((HALF, 8, 128), F32),
        vm((NC, 8, 128), F32), vm((HALF, 8, 128), F32), vm((NO, 2, HALF, 8, 128), F32),
        vm((PROJ, PROJ), F32),
        vm((NO, 2, ORB, BLOCK), F32), vm((NO, 2, ORB, BLOCK), F32),
        vm((PROJ, BLOCK), F32), vm((ORB, NO * BLOCK), F32), vm((ORB, NO * BLOCK), F32),
        dma((4,)), dma((2,)), dma((2,)), dma((6, 2)), dma((6, 2)), dma((6, 2)),
        dma((NO,)), dma((NO,)), dma((NO,)), dma((NO,)),
        dma((NC,)), dma((NC,)), dma((NC,)), dma((NC,)),
        dma((NO,)), dma((NO,)), dma((NO,)), dma((NO,)), dma((2,)), dma((2,)), dma((NO,)), dma((NO,)),
    ]
    return pl.pallas_call(
        kernel,
        out_shape=jax.ShapeDtypeStruct(field, F32),
        in_specs=[pl.BlockSpec(memory_space=pl.ANY)] * 3,
        out_specs=pl.BlockSpec(memory_space=pltpu.VMEM),
        scratch_shapes=scratch,
        compiler_params=pltpu.CompilerParams(
            collective_id=0, has_side_effects=True, vmem_limit_bytes=56 * 1024 * 1024
        ),
    )(orbitals, potential, projectors)


def solution(mesh):
    placed = (P("grid", "orb", None), P("grid", None), P("grid", None, "orb"))
    return jax.shard_map(
        shards, mesh=mesh, in_specs=placed, out_specs=P("grid", "orb", None), check_vma=False
    )
```
